32 devices in a mesh: rows: 4 (over y, x), cols: 8 (over z, core).
Axes of the slice: x: 2, y: 2, z: 4, core: 2. Of those that a mesh axis runs over, the one named last changes fastest.
Arguments:
- pixels: bfloat16 [128, 256, 768], P('rows', 'cols'), may hold values from -6 to 6
- tissue: int32 [128, 256], P('rows', 'cols'), may hold values 0 or 1
- patch_weight: bfloat16 [768, 1024], replicated, may hold values from -0.21875 to 0.21875
- conv_weight: bfloat16 [9, 32, 1024], replicated, may hold values from -0.375 to 0.375
- kv_weight: bfloat16 [1024, 2048], replicated, may hold values from -0.1875 to 0.1875
- query_weight: bfloat16 [1024, 1024], replicated, may hold values from -0.1875 to 0.1875
- out_weight: bfloat16 [1024, 1024], replicated, may hold values from -0.1875 to 0.1875
- latents: bfloat16 [512, 1024], replicated, may hold values from -240 to 240
Outputs:
- features: bfloat16 [128, 256, 1024], P('rows', 'cols')
- latents_out: bfloat16 [512, 1024], P(('rows', 'cols'))
The draws below stay inside these ranges and needn't reach their ends.
Inputs may be any that keep to these rules, and one draw needn't show every extreme that they name: 1 marks a patch tile that holds tissue, and at least one tile of the slab holds tissue.
All inputs are finite; a program needn't handle non-finite values. No bound on the sum of `tissue` on one device may be relied on, other than what follows from the above.
Results may differ from the reference program's by a relative error of at most 0.03.
Values may be sent and summed in bfloat16 or wider, within the bound.
A program may use at most 128 MiB of HBM per device.

```python
import jax
import jax.numpy as jnp
from jax import lax

D = 1024
HEADS = 16
LAT = 512
PATCH_IN = 768
NR = 128
NC = 256
GW = 32


def draw_latents(key, part):
    first_key = jax.random.fold_in(key, 0)
    drawn = jax.random.normal(first_key, (LAT, D), jnp.float32)
    drawn = jnp.clip(drawn, -6.0, 6.0)
    return drawn.astype(jnp.bfloat16)


def touch_ends(values, own_key, smallest, high):
    extent = values.shape
    index_at = [jax.random.randint(jax.random.fold_in(own_key, axis), (), 0, extent[axis]) for axis in range(len(extent))]
    values = values.at[tuple(index_at)].set(smallest)
    longest = extent.index(max(extent))
    index_at[longest] = (index_at[longest] + 1) % extent[longest]
    return values.at[tuple(index_at)].set(high)


def block_scale(stream_key, dims, cuts, least, largest):
    gain = 1.0
    for position, blocks in cuts:
        steps = jax.random.uniform(jax.random.fold_in(jax.random.fold_in(stream_key, 6), position), (blocks,), jnp.float32, least / len(cuts), largest / len(cuts))
        gain = gain * jnp.repeat(jnp.exp(steps), dims[position] // blocks).reshape((-1,) + (1,) * (len(dims) - 1 - position))
    return gain


def gaussian(rng, extent, width, bound, pieces=(), kind=jnp.bfloat16):
    result = jax.random.normal(rng, extent, jnp.float32) * width
    if len(pieces) > 0:
        result = block_scale(rng, extent, pieces, -0.22, 0.18) * result
    return jnp.clip(result, min=-bound, max=bound).astype(kind)


def setup_inputs(seed: int = 0) -> dict:
    key_of = jax.random.split(jax.random.key(seed), 9)
    pixels = gaussian(key_of[0], (NR, NC, PATCH_IN), 1.0, 6.0, ((0, 4), (1, 8)))
    tissue = touch_ends((jax.random.randint(key_of[1], (NR, NC), 0, 5) < 3).astype(jnp.int32), jax.random.fold_in(key_of[1], 1), 0, 1)
    patch_weight = gaussian(key_of[2], (PATCH_IN, D), PATCH_IN ** -0.5, 0.21875)
    conv_weight = gaussian(key_of[3], (9, GW, D), (9 * GW) ** -0.5, 0.375)
    kv_weight = gaussian(key_of[4], (D, 2 * D), D ** -0.5, 0.1875)
    query_weight = gaussian(key_of[5], (D, D), D ** -0.5, 0.1875)
    out_weight = gaussian(key_of[6], (D, D), D ** -0.5, 0.1875)
    latents = draw_latents(jax.random.fold_in(key_of[8], 71), 0)
    return dict(pixels=pixels, tissue=tissue, patch_weight=patch_weight, conv_weight=conv_weight, kv_weight=kv_weight, query_weight=query_weight, out_weight=out_weight, latents=latents)


def reference(pixels, tissue, patch_weight, conv_weight, kv_weight, query_weight, out_weight, latents):
    rows_all, cols_all, patch_in = pixels.shape
    channels = patch_weight.shape[1]
    token_count = rows_all * cols_all
    embedded = jnp.dot(pixels.reshape(token_count, patch_in), patch_weight, preferred_element_type=jnp.float32)
    embedded = embedded.astype(jnp.bfloat16).reshape(rows_all, cols_all, channels)
    padded = jnp.pad(embedded, ((1, 1), (1, 1), (0, 0)))
    group_width = conv_weight.shape[1]
    group_count = channels // group_width
    kernel = conv_weight.astype(jnp.float32).reshape(9, group_width, group_count, group_width)
    convolved = jnp.zeros((rows_all, cols_all, group_count, group_width), jnp.float32)
    for row_shift in range(3):
        for col_shift in range(3):
            window = padded[row_shift:row_shift + rows_all, col_shift:col_shift + cols_all]
            window = window.astype(jnp.float32).reshape(rows_all, cols_all, group_count, group_width)
            convolved = convolved + jnp.einsum('hwgi,igo->hwgo', window, kernel[3 * row_shift + col_shift])
    summed = embedded.astype(jnp.float32) + convolved.reshape(rows_all, cols_all, channels)
    average = lax.optimization_barrier(jnp.mean(summed, axis=-1, keepdims=True))
    centred = summed - average
    variance = lax.optimization_barrier(jnp.mean(centred * centred, axis=-1, keepdims=True))
    features = (centred * lax.rsqrt(variance + 1e-05)).astype(jnp.bfloat16)
    projected = jnp.dot(features.reshape(token_count, channels), kv_weight, preferred_element_type=jnp.float32).astype(jnp.bfloat16)
    head_dim = channels // HEADS
    key_vectors = projected[:, :channels].reshape(token_count, HEADS, head_dim).transpose(1, 0, 2)
    value_vectors = projected[:, channels:].reshape(token_count, HEADS, head_dim).transpose(1, 0, 2)
    queries = jnp.dot(latents, query_weight, preferred_element_type=jnp.float32).astype(jnp.bfloat16)
    latent_count = latents.shape[0]
    queries = queries.reshape(latent_count, HEADS, head_dim).transpose(1, 0, 2)
    tissue_live = tissue.reshape(token_count) > 0

    def one_head(operands):
        query_head, key_head, value_head = operands
        scores = jnp.dot(query_head, key_head.T, preferred_element_type=jnp.float32) * head_dim ** (-0.5)
        scores = jnp.where(tissue_live[None, :], scores, -1e+30)
        highest = lax.optimization_barrier(jnp.max(scores, axis=1, keepdims=True))
        weights = jnp.where(tissue_live[None, :], jnp.exp(scores - highest), 0.0)
        denominator = lax.optimization_barrier(jnp.sum(weights, axis=1, keepdims=True))
        numerator = jnp.dot(weights.astype(jnp.bfloat16), value_head, preferred_element_type=jnp.float32)
        return numerator / denominator
    attended = lax.map(one_head, (queries, key_vectors, value_vectors))
    attended = attended.transpose(1, 0, 2).reshape(latent_count, channels)
    normed = (attended * lax.rsqrt(lax.optimization_barrier(jnp.mean(attended * attended, axis=-1, keepdims=True)) + 1e-06)).astype(jnp.bfloat16)
    latents_out = jnp.dot(normed, out_weight, preferred_element_type=jnp.float32).astype(jnp.bfloat16)
    return (features, latents_out)
```

```python
import functools

import jax
import jax.numpy as jnp
from jax import lax
from jax.experimental import pallas as pl
from jax.experimental.pallas import tpu as pltpu
from jax.sharding import PartitionSpec as P

HEADS = 16
BLOCK = 256
LANES = 128
PAD = 8
F32 = jnp.float32
BF16 = jnp.bfloat16
LOW = -1e30


def dot(a, b):
    return jnp.dot(a, b, preferred_element_type=F32)


def shifted(cells, axis, step):
    count = lax.axis_size(axis)
    pairs = [(i, i + step) for i in range(count) if 0 <= i + step < count]
    return lax.ppermute(cells, axis, pairs)


def core(
    tile_rows, tile_cols, heads,
    main_ref, top_ref, bottom_ref, side_ref, live_ref, patch_ref, conv_ref, kv_ref, query_ref,
    features_ref, part_ref, stat_ref,
    wide_ref, taps_ref, summed_ref, keys_ref,
):
    tokens = tile_rows * tile_cols
    channels = patch_ref.shape[1]
    group = conv_ref.shape[1]
    rows_ext = tile_rows + 2
    col_ext = tile_cols + PAD
    same = (
        lax.broadcasted_iota(jnp.int32, (BLOCK, BLOCK), 0) // group
        == lax.broadcasted_iota(jnp.int32, (BLOCK, BLOCK), 1) // group
    )
    for block in range(channels // BLOCK):
        lanes = slice(block * BLOCK, (block + 1) * BLOCK)
        patch = patch_ref[:, lanes]
        inner = jnp.concatenate(
            [dot(top_ref[...], patch), dot(main_ref[...], patch), dot(bottom_ref[...], patch)], 0
        )
        side = dot(side_ref[...], patch)
        full = jnp.concatenate(
            [inner.reshape(rows_ext, tile_cols, BLOCK), side.reshape(rows_ext, PAD, BLOCK)], 1
        ).reshape(rows_ext * col_ext, BLOCK)
        for col_shift, amount in ((0, 1), (2, rows_ext * col_ext - 1)):
            moved = pltpu.roll(full, amount, 0).reshape(rows_ext, col_ext, BLOCK)
            moved = moved[:, :tile_cols].reshape(rows_ext * tile_cols, BLOCK)
            wide_ref[:, col_shift * BLOCK : (col_shift + 1) * BLOCK] = moved.astype(BF16)
        wide_ref[:, BLOCK : 2 * BLOCK] = inner.astype(BF16)
        for tap in range(9):
            small = conv_ref[tap, :, lanes]
            tiled = jnp.concatenate([small] * (BLOCK // group), 0)
            row_shift, col_shift = tap // 3, tap % 3
            taps_ref[row_shift, col_shift * BLOCK : (col_shift + 1) * BLOCK, :] = jnp.where(
                same, tiled, jnp.zeros_like(tiled)
            )
        total = wide_ref[tile_cols : tile_cols + tokens, BLOCK : 2 * BLOCK].astype(F32)
        for row_shift in range(3):
            first = row_shift * tile_cols
            total = total + dot(wide_ref[first : first + tokens, :], taps_ref[row_shift])
        summed_ref[:, lanes] = total

    chunk = 128
    inverse = 1.0 / channels

    def normalise(step, _):
        at = pl.ds(pl.multiple_of(step * chunk, chunk), chunk)
        values = summed_ref[at, :]
        centred = values - jnp.sum(values, axis=-1, keepdims=True) * inverse
        variance = jnp.sum(centred * centred, axis=-1, keepdims=True) * inverse
        features_ref[at, :] = (centred * lax.rsqrt(variance + 1e-05)).astype(BF16)
        return 0

    lax.fori_loop(0, tokens // chunk, normalise, 0)

    def project(step, _):
        at = pl.ds(pl.multiple_of(step * BLOCK, BLOCK), BLOCK)
        keys_ref[:, at] = dot(features_ref[...], kv_ref[:, at]).astype(BF16)
        return 0

    lax.fori_loop(0, keys_ref.shape[1] // BLOCK, project, 0)

    latent_count = query_ref.shape[0]
    head_dim = channels // heads
    token_lane = lax.broadcasted_iota(jnp.int32, (tokens, LANES), 1)
    query_lane = lax.broadcasted_iota(jnp.int32, (latent_count, LANES), 1)
    token_low = token_lane < head_dim
    query_low = query_lane < head_dim
    stat_ref[...] = jnp.zeros_like(stat_ref)

    def attend(pair, _):
        at = pl.ds(pl.multiple_of(pair * LANES, LANES), LANES)
        value_at = pl.ds(pl.multiple_of(channels + pair * LANES, LANES), LANES)
        queries = query_ref[:, at]
        keys = keys_ref[:, at]
        values = keys_ref[:, value_at]
        live = live_ref[...]
        bias = (live - 1.0) * (-LOW)
        bias = bias.astype(BF16)
        ones = jnp.ones_like(values)
        results = []
        stats = stat_ref[...]
        for which in range(2):
            query_mine = query_low if which == 0 else jnp.logical_not(query_low)
            token_mine = token_low if which == 0 else jnp.logical_not(token_low)
            spot = head_dim if which == 0 else 0
            marker = (query_lane == spot).astype(F32).astype(BF16)
            query_head = jnp.where(query_mine, queries, marker)
            key_head = jnp.where(token_mine, keys, bias)
            value_head = jnp.where(token_mine, values, ones) * live
            scores = lax.dot_general(
                query_head, key_head, (((1,), (1,)), ((), ())), preferred_element_type=F32
            )
            peak = jnp.max(scores, axis=1, keepdims=True)
            weights = jnp.exp(scores - peak).astype(BF16)
            got = dot(weights, value_head)
            results.append(got)
            head = pair * 2 + which
            total = got[:, spot : spot + 1]
            stats = jnp.where(query_lane == head, peak, stats)
            stats = jnp.where(query_lane == head_dim + head, total, stats)
        stat_ref[...] = stats
        numer = jnp.where(query_low, results[0], results[1])
        denom = jnp.where(query_low, results[1], results[0])
        denom = pltpu.roll(denom, head_dim, 1)
        part_ref[:, at] = jnp.where(denom > 0, numer / jnp.maximum(denom, 1e-30), 0.0).astype(BF16)
        return 0

    lax.fori_loop(0, heads // 2, attend, 0)


def local_work(pixels, top, bottom, side, live, patch_weight, conv_weight, kv_weight, queries):
    tile_rows, tile_cols, patch_in = pixels.shape
    channels = patch_weight.shape[1]
    tokens = tile_rows * tile_cols
    latent_count = queries.shape[0]
    rows_ext = tile_rows + 2
    vmem = pl.BlockSpec(memory_space=pltpu.VMEM)
    return pl.pallas_call(
        functools.partial(core, tile_rows, tile_cols, HEADS),
        out_shape=(
            jax.ShapeDtypeStruct((tokens, channels), BF16),
            jax.ShapeDtypeStruct((latent_count, channels), BF16),
            jax.ShapeDtypeStruct((latent_count, LANES), F32),
        ),
        in_specs=[vmem] * 9,
        out_specs=(vmem, vmem, vmem),
        scratch_shapes=[
            pltpu.VMEM((rows_ext * tile_cols, 3 * BLOCK), BF16),
            pltpu.VMEM((3, 3 * BLOCK, BLOCK), BF16),
            pltpu.VMEM((tokens, channels), F32),
            pltpu.VMEM((tokens, 2 * channels), BF16),
        ],
        compiler_params=pltpu.CompilerParams(vmem_limit_bytes=58 * 1024 * 1024),
        name="local_work",
    )(
        pixels.reshape(tokens, patch_in), top, bottom,
        side.reshape(rows_ext * PAD, patch_in), live, patch_weight, conv_weight, kv_weight, queries,
    )


def shards(pixels, tissue, patch_weight, conv_weight, kv_weight, query_weight, out_weight, latents):
    tile_rows, tile_cols, patch_in = pixels.shape
    channels = patch_weight.shape[1]
    tokens = tile_rows * tile_cols
    head_dim = channels // HEADS
    latent_count = latents.shape[0]
    top = shifted(pixels[-1:], "rows", 1)
    bottom = shifted(pixels[:1], "rows", -1)
    first = jnp.concatenate([top[:, :1], pixels[:, :1], bottom[:, :1]], 0)
    last = jnp.concatenate([top[:, -1:], pixels[:, -1:], bottom[:, -1:]], 0)
    left = shifted(last, "cols", 1)
    right = shifted(first, "cols", -1)
    side = jnp.concatenate(
        [right, jnp.zeros((tile_rows + 2, PAD - 2, patch_in), BF16), jnp.roll(left, -1, 0)], 1
    )
    queries = (dot(latents, query_weight).astype(BF16) * (head_dim ** -0.5)).astype(BF16)
    live = jnp.broadcast_to((tissue.reshape(tokens, 1) > 0).astype(BF16), (tokens, LANES))
    features, part, stat = local_work(
        pixels, top[0], bottom[0], side, live, patch_weight, conv_weight, kv_weight, queries
    )
    devices = lax.axis_size(("rows", "cols"))
    own = latent_count // devices
    swap = functools.partial(
        lax.all_to_all, axis_name=("rows", "cols"), split_axis=1, concat_axis=0, tiled=True
    )
    got = swap(part[None]).reshape(devices, own, HEADS, head_dim).astype(F32)
    stats = swap(stat[None])
    peak = stats[:, :, :HEADS]
    total = stats[:, :, head_dim : head_dim + HEADS]
    factor = jnp.exp(peak - jnp.max(peak, axis=0)[None]) * total
    factor = factor / jnp.sum(factor, axis=0)[None]
    attended = jnp.sum(got * factor[:, :, :, None], axis=0).reshape(own, channels)
    normed = attended * lax.rsqrt(jnp.mean(attended * attended, axis=-1, keepdims=True) + 1e-06)
    latents_out = dot(normed.astype(BF16), out_weight).astype(BF16)
    return (features.reshape(tile_rows, tile_cols, channels), latents_out)


def solution(mesh):
    return jax.shard_map(
        shards,
        mesh=mesh,
        in_specs=(P("rows", "cols", None), P("rows", "cols"), P(), P(), P(), P(), P(), P()),
        out_specs=(P("rows", "cols", None), P(("rows", "cols"), None)),
        check_vma=False,
    )
```

```python
import functools

import jax
import jax.numpy as jnp
from jax import lax
from jax.experimental import pallas as pl
from jax.experimental.pallas import tpu as pltpu
from jax.sharding import PartitionSpec as P

HEADS = 16
BLOCK = 256
LANES = 128
PAD = 8
F32 = jnp.float32
BF16 = jnp.bfloat16
LOW = -1e30


def dot(a, b):
    return jnp.dot(a, b, preferred_element_type=F32)


def shifted(cells, axis, step):
    count = lax.axis_size(axis)
    pairs = [(i, i + step) for i in range(count) if 0 <= i + step < count]
    return lax.ppermute(cells, axis, pairs)


def core(
    tile_rows, tile_cols, heads,
    main_ref, top_ref, bottom_ref, side_ref, live_ref, patch_ref, conv_ref, kv_ref, query_ref,
    features_ref, part_ref, stat_ref,
    wide_ref, taps_ref, summed_ref, keys_ref,
):
    tokens = tile_rows * tile_cols
    channels = patch_ref.shape[1]
    group = conv_ref.shape[1]
    rows_ext = tile_rows + 2
    col_ext = tile_cols + PAD
    same = (
        lax.broadcasted_iota(jnp.int32, (BLOCK, BLOCK), 0) // group
        == lax.broadcasted_iota(jnp.int32, (BLOCK, BLOCK), 1) // group
    )
    for block in range(channels // BLOCK):
        lanes = slice(block * BLOCK, (block + 1) * BLOCK)
        patch = patch_ref[:, lanes]
        inner = jnp.concatenate(
            [dot(top_ref[...], patch), dot(main_ref[...], patch), dot(bottom_ref[...], patch)], 0
        )
        side = dot(side_ref[...], patch)
        full = jnp.concatenate(
            [inner.reshape(rows_ext, tile_cols, BLOCK), side.reshape(rows_ext, PAD, BLOCK)], 1
        ).reshape(rows_ext * col_ext, BLOCK)
        for col_shift, amount in ((0, 1), (2, rows_ext * col_ext - 1)):
            moved = pltpu.roll(full, amount, 0).reshape(rows_ext, col_ext, BLOCK)
            moved = moved[:, :tile_cols].reshape(rows_ext * tile_cols, BLOCK)
            wide_ref[:, col_shift * BLOCK : (col_shift + 1) * BLOCK] = moved.astype(BF16)
        wide_ref[:, BLOCK : 2 * BLOCK] = inner.astype(BF16)
        for tap in range(9):
            small = conv_ref[tap, :, lanes]
            tiled = jnp.concatenate([small] * (BLOCK // group), 0)
            row_shift, col_shift = tap // 3, tap % 3
            taps_ref[row_shift, col_shift * BLOCK : (col_shift + 1) * BLOCK, :] = jnp.where(
                same, tiled, jnp.zeros_like(tiled)
            )
        total = wide_ref[tile_cols : tile_cols + tokens, BLOCK : 2 * BLOCK].astype(F32)
        for row_shift in range(3):
            first = row_shift * tile_cols
            total = total + dot(wide_ref[first : first + tokens, :], taps_ref[row_shift])
        summed_ref[:, lanes] = total

    chunk = 128
    inverse = 1.0 / channels

    def normalise(step, _):
        at = pl.ds(pl.multiple_of(step * chunk, chunk), chunk)
        values = summed_ref[at, :]
        centred = values - jnp.sum(values, axis=-1, keepdims=True) * inverse
        variance = jnp.sum(centred * centred, axis=-1, keepdims=True) * inverse
        features_ref[at, :] = (centred * lax.rsqrt(variance + 1e-05)).astype(BF16)
        return 0

    lax.fori_loop(0, tokens // chunk, normalise, 0)

    def project(step, _):
        at = pl.ds(pl.multiple_of(step * BLOCK, BLOCK), BLOCK)
        keys_ref[:, at] = dot(features_ref[...], kv_ref[:, at]).astype(BF16)
        return 0

    lax.fori_loop(0, keys_ref.shape[1] // BLOCK, project, 0)

    latent_count = query_ref.shape[0]
    head_dim = channels // heads
    token_lane = lax.broadcasted_iota(jnp.int32, (tokens, LANES), 1)
    query_lane = lax.broadcasted_iota(jnp.int32, (latent_count, LANES), 1)
    token_low = token_lane < head_dim
    query_low = query_lane < head_dim
    stat_ref[...] = jnp.zeros_like(stat_ref)

    def attend(pair, _):
        at = pl.ds(pl.multiple_of(pair * LANES, LANES), LANES)
        value_at = pl.ds(pl.multiple_of(channels + pair * LANES, LANES), LANES)
        queries = query_ref[:, at]
        keys = keys_ref[:, at]
        values = keys_ref[:, value_at]
        live = live_ref[...]
        bias = (live - 1.0) * (-LOW)
        bias = bias.astype(BF16)
        ones = jnp.ones_like(values)
        results = []
        stats = stat_ref[...]
        for which in range(2):
            query_mine = query_low if which == 0 else jnp.logical_not(query_low)
            token_mine = token_low if which == 0 else jnp.logical_not(token_low)
            spot = head_dim if which == 0 else 0
            marker = (query_lane == spot).astype(F32).astype(BF16)
            query_head = jnp.where(query_mine, queries, marker)
            key_head = jnp.where(token_mine, keys, bias)
            value_head = jnp.where(token_mine, values, ones) * live
            scores = lax.dot_general(
                query_head, key_head, (((1,), (1,)), ((), ())), preferred_element_type=F32
            )
            peak = jnp.max(scores, axis=1, keepdims=True)
            weights = jnp.exp(scores - peak).astype(BF16)
            got = dot(weights, value_head)
            results.append(got)
            head = pair * 2 + which
            total = got[:, spot : spot + 1]
            stats = jnp.where(query_lane == head, peak, stats)
            stats = jnp.where(query_lane == head_dim + head, total, stats)
        stat_ref[...] = stats
        numer = jnp.where(query_low, results[0], results[1])
        denom = jnp.where(query_low, results[1], results[0])
        denom = pltpu.roll(denom, head_dim, 1)
        part_ref[:, at] = jnp.where(denom > 0, numer / jnp.maximum(denom, 1e-30), 0.0).astype(BF16)
        return 0

    lax.fori_loop(0, heads // 2, attend, 0)


def local_work(pixels, top, bottom, side, live, patch_weight, conv_weight, kv_weight, queries):
    tile_rows, tile_cols, patch_in = pixels.shape
    channels = patch_weight.shape[1]
    tokens = tile_rows * tile_cols
    latent_count = queries.shape[0]
    rows_ext = tile_rows + 2
    vmem = pl.BlockSpec(memory_space=pltpu.VMEM)
    return pl.pallas_call(
        functools.partial(core, tile_rows, tile_cols, HEADS),
        out_shape=(
            jax.ShapeDtypeStruct((tokens, channels), BF16),
            jax.ShapeDtypeStruct((latent_count, channels), BF16),
            jax.ShapeDtypeStruct((latent_count, LANES), F32),
        ),
        in_specs=[vmem] * 9,
        out_specs=(vmem, vmem, vmem),
        scratch_shapes=[
            pltpu.VMEM((rows_ext * tile_cols, 3 * BLOCK), BF16),
            pltpu.VMEM((3, 3 * BLOCK, BLOCK), BF16),
            pltpu.VMEM((tokens, channels), F32),
            pltpu.VMEM((tokens, 2 * channels), BF16),
        ],
        compiler_params=pltpu.CompilerParams(vmem_limit_bytes=40 * 1024 * 1024),
        name="local_work",
    )(
        pixels.reshape(tokens, patch_in), top, bottom,
        side.reshape(rows_ext * PAD, patch_in), live, patch_weight, conv_weight, kv_weight, queries,
    )


MESH = pl.DeviceIdType.MESH


def spread(values, heads, head_dim, low):
    return [
        jnp.where(low, values[:, 2 * pair : 2 * pair + 1], values[:, 2 * pair + 1 : 2 * pair + 2])
        for pair in range(heads // 2)
    ]


def blend(parts, stats, heads, head_dim):
    rows = parts[0].shape[0]
    lane = lax.broadcasted_iota(jnp.int32, (rows, LANES), 1)
    low = lane < head_dim
    peaks = stats
    totals = [pltpu.roll(stat, LANES - head_dim, 1) for stat in stats]
    top = functools.reduce(jnp.maximum, peaks)
    shares = [jnp.exp(peak - top) * total for peak, total in zip(peaks, totals)]
    whole = functools.reduce(jnp.add, shares)
    inverse = jnp.where(whole > 0, 1.0 / jnp.maximum(whole, 1e-30), 0.0)
    columns = [0.0] * (heads // 2)
    for part, share in zip(parts, shares):
        factors = spread(share * inverse, heads, head_dim, low)
        for pair in range(heads // 2):
            piece = part[:, pair * LANES : (pair + 1) * LANES].astype(F32)
            columns[pair] = columns[pair] + factors[pair] * piece
    used = lane < heads
    stat = jnp.where(used, top, 0.0)
    stat = jnp.where(lane < head_dim, stat, pltpu.roll(jnp.where(used, whole, 0.0), head_dim, 1))
    return columns, stat


def exchange(
    heads,
    part_ref, stat_ref, weight_hbm,
    out_ref,
    part_one, stat_one, sum_one, tot_one, part_two, stat_two, sum_two, tot_two,
    part_three, stat_three, weight_ref, send_sem, recv_sem, load_sem,
):
    row_count, half, _, own, channels = part_ref.shape
    head_dim = channels // heads
    row = lax.axis_index("rows")
    col = lax.axis_index("cols")
    side = lax.rem(col, 2)
    slot = lax.div(col, 2)
    load = pltpu.make_async_copy(weight_hbm, weight_ref, load_sem)
    load.start()

    twin = (row, slot * 2 + (1 - side))
    row_peers = [(lax.rem(row + step, row_count), col) for step in range(1, row_count)]
    col_peers = [(row, lax.rem(slot + step, half) * 2 + side) for step in range(1, half)]
    barrier = pltpu.get_barrier_semaphore()
    for peer in [twin] + row_peers + col_peers:
        pl.semaphore_signal(barrier, inc=1, device_id=peer, device_id_type=MESH)
    pl.semaphore_wait(barrier, 1 + len(row_peers) + len(col_peers))

    def send(source, target, peer, number):
        copy = pltpu.make_async_remote_copy(
            src_ref=source, dst_ref=target,
            send_sem=send_sem.at[number], recv_sem=recv_sem.at[number],
            device_id=peer, device_id_type=MESH,
        )
        copy.start()
        return copy

    copies = [
        send(part_ref.at[:, :, 1 - side], part_one, twin, 0),
        send(stat_ref.at[:, :, 1 - side], stat_one, twin, 1),
    ]
    for copy in copies:
        copy.wait()

    def first(index, _):
        a, b = lax.div(index, half), lax.rem(index, half)
        columns, stat = blend(
            [part_ref[a, b, side], part_one[a, b]], [stat_ref[a, b, side], stat_one[a, b]],
            heads, head_dim,
        )
        for pair, column in enumerate(columns):
            sum_one[a, b, :, pair * LANES : (pair + 1) * LANES] = column.astype(BF16)
        tot_one[a, b] = stat
        return 0

    lax.fori_loop(0, row_count * half, first, 0)

    copies = []
    for step, peer in enumerate(row_peers):
        number = 2 + 2 * step
        copies.append(send(sum_one.at[peer[0]], part_two.at[step], peer, number))
        copies.append(send(tot_one.at[peer[0]], stat_two.at[step], peer, number + 1))
    for copy in copies:
        copy.wait()

    def second(b, _):
        columns, stat = blend(
            [sum_one[row, b]] + [part_two[step, b] for step in range(row_count - 1)],
            [tot_one[row, b]] + [stat_two[step, b] for step in range(row_count - 1)],
            heads, head_dim,
        )
        for pair, column in enumerate(columns):
            sum_two[b, :, pair * LANES : (pair + 1) * LANES] = column.astype(BF16)
        tot_two[b] = stat
        return 0

    lax.fori_loop(0, half, second, 0)

    copies = []
    for step, peer in enumerate(col_peers):
        number = 2 * row_count + 2 * step
        where = lax.rem(slot + step + 1, half)
        copies.append(send(sum_two.at[where], part_three.at[step], peer, number))
        copies.append(send(tot_two.at[where], stat_three.at[step], peer, number + 1))
    for copy in copies:
        copy.wait()
    columns, _ = blend(
        [sum_two[slot]] + [part_three[step] for step in range(half - 1)],
        [tot_two[slot]] + [stat_three[step] for step in range(half - 1)],
        heads, head_dim,
    )
    attended = jnp.concatenate(columns, 1)
    mean = jnp.sum(attended * attended, axis=-1, keepdims=True) * (1.0 / channels)
    normed = (attended * lax.rsqrt(mean + 1e-06)).astype(BF16)
    load.wait()
    out_ref[...] = dot(normed, weight_ref[...]).astype(BF16)


def combine(part, stat, out_weight):
    row_count, col_count = lax.axis_size("rows"), lax.axis_size("cols")
    half = col_count // 2
    latent_count, channels = part.shape
    own = latent_count // (row_count * col_count)
    part = part.reshape(row_count, half, 2, own, channels)
    stat = stat.reshape(row_count, half, 2, own, LANES)
    vmem = pl.BlockSpec(memory_space=pltpu.VMEM)
    copies = 2 + 2 * (row_count - 1) + 2 * (half - 1)

    def pairs(*extent):
        return [
            pltpu.VMEM(extent + (own, channels), BF16), pltpu.VMEM(extent + (own, LANES), F32)
        ]

    return pl.pallas_call(
        functools.partial(exchange, HEADS),
        out_shape=jax.ShapeDtypeStruct((own, out_weight.shape[1]), BF16),
        in_specs=[vmem, vmem, pl.BlockSpec(memory_space=pl.ANY)],
        out_specs=vmem,
        scratch_shapes=pairs(row_count, half)
        + pairs(row_count, half)
        + pairs(row_count - 1, half)
        + pairs(half)
        + pairs(half - 1)
        + [
            pltpu.VMEM(out_weight.shape, BF16),
            pltpu.SemaphoreType.DMA((copies,)),
            pltpu.SemaphoreType.DMA((copies,)),
            pltpu.SemaphoreType.DMA,
        ],
        compiler_params=pltpu.CompilerParams(
            collective_id=1, has_side_effects=True, vmem_limit_bytes=24 * 1024 * 1024
        ),
        name="combine",
    )(part, stat, out_weight)


def shards(pixels, tissue, patch_weight, conv_weight, kv_weight, query_weight, out_weight, latents):
    tile_rows, tile_cols, patch_in = pixels.shape
    channels = patch_weight.shape[1]
    tokens = tile_rows * tile_cols
    head_dim = channels // HEADS
    latent_count = latents.shape[0]
    top = shifted(pixels[-1:], "rows", 1)
    bottom = shifted(pixels[:1], "rows", -1)
    first = jnp.concatenate([top[:, :1], pixels[:, :1], bottom[:, :1]], 0)
    last = jnp.concatenate([top[:, -1:], pixels[:, -1:], bottom[:, -1:]], 0)
    left = shifted(last, "cols", 1)
    right = shifted(first, "cols", -1)
    side = jnp.concatenate(
        [right, jnp.zeros((tile_rows + 2, PAD - 2, patch_in), BF16), jnp.roll(left, -1, 0)], 1
    )
    queries = (dot(latents, query_weight).astype(BF16) * (head_dim ** -0.5)).astype(BF16)
    live = jnp.broadcast_to((tissue.reshape(tokens, 1) > 0).astype(BF16), (tokens, LANES))
    features, part, stat = local_work(
        pixels, top[0], bottom[0], side, live, patch_weight, conv_weight, kv_weight, queries
    )
    latents_out = combine(part, stat, out_weight)
    return (features.reshape(tile_rows, tile_cols, channels), latents_out)


def solution(mesh):
    return jax.shard_map(
        shards,
        mesh=mesh,
        in_specs=(P("rows", "cols", None), P("rows", "cols"), P(), P(), P(), P(), P(), P()),
        out_specs=(P("rows", "cols", None), P(("rows", "cols"), None)),
        check_vma=False,
    )
```

```python
import functools

import jax
import jax.numpy as jnp
from jax import lax
from jax.experimental import pallas as pl
from jax.experimental.pallas import tpu as pltpu
from jax.sharding import PartitionSpec as P

HEADS = 16
BLOCK = 256
LANES = 128
PAD = 8
CORNER = 16
F32 = jnp.float32
BF16 = jnp.bfloat16
LOW = -1e30
MESH = pl.DeviceIdType.MESH


def dot(a, b):
    return jnp.dot(a, b, preferred_element_type=F32)


def core(
    tile_rows, tile_cols, heads,
    top_ref, bottom_ref, left_ref, right_ref, live_ref,
    main_hbm, patch_hbm, conv_hbm, latent_hbm, weight_hbm, kv_hbm,
    part_ref, stat_ref, features_hbm,
    main_ref, patch_ref, conv_ref, latent_ref, weight_ref, kv_ref,
    wide_ref, taps_ref, summed_ref, keys_ref, query_ref, features_ref, load_sem,
):
    loads = [
        pltpu.make_async_copy(source, target, load_sem.at[number])
        for number, (source, target) in enumerate(
            (
                (main_hbm, main_ref), (patch_hbm, patch_ref), (conv_hbm, conv_ref),
                (latent_hbm, latent_ref), (weight_hbm, weight_ref), (kv_hbm, kv_ref),
            )
        )
    ]
    for load in loads:
        load.start()
    tokens = tile_rows * tile_cols
    channels = patch_ref.shape[1]
    group = conv_ref.shape[1]
    rows_ext = tile_rows + 2
    col_ext = tile_cols + PAD
    same = (
        lax.broadcasted_iota(jnp.int32, (BLOCK, BLOCK), 0) // group
        == lax.broadcasted_iota(jnp.int32, (BLOCK, BLOCK), 1) // group
    )
    side_slot = lax.broadcasted_iota(jnp.int32, (rows_ext, PAD, BLOCK), 1)
    tall = (1, PAD, BLOCK)

    def border(values, upper, lower):
        return (
            jnp.broadcast_to(values[upper : upper + 1][:, None, :], tall),
            jnp.broadcast_to(values[:tile_rows][:, None, :], (tile_rows, PAD, BLOCK)),
            jnp.broadcast_to(values[lower : lower + 1][:, None, :], tall),
        )

    for load in loads[:3]:
        load.wait()
    for block in range(channels // BLOCK):
        lanes = slice(block * BLOCK, (block + 1) * BLOCK)
        patch = patch_ref[:, lanes]
        inner = jnp.concatenate(
            [dot(top_ref[...], patch), dot(main_ref[...], patch), dot(bottom_ref[...], patch)], 0
        )
        upper, middle, lower = border(
            dot(left_ref[...], patch), tile_rows + CORNER - 1, tile_rows + 2 * CORNER - 1
        )
        from_left = jnp.concatenate([middle, lower, upper], 0)
        upper, middle, lower = border(
            dot(right_ref[...], patch), tile_rows, tile_rows + CORNER
        )
        from_right = jnp.concatenate([upper, middle, lower], 0)
        side = jnp.where(side_slot == PAD - 1, from_left, from_right)
        full = jnp.concatenate(
            [inner.reshape(rows_ext, tile_cols, BLOCK), side], 1
        ).reshape(rows_ext * col_ext, BLOCK)
        for col_shift, amount in ((0, 1), (2, rows_ext * col_ext - 1)):
            moved = pltpu.roll(full, amount, 0).reshape(rows_ext, col_ext, BLOCK)
            moved = moved[:, :tile_cols].reshape(rows_ext * tile_cols, BLOCK)
            wide_ref[:, col_shift * BLOCK : (col_shift + 1) * BLOCK] = moved.astype(BF16)
        wide_ref[:, BLOCK : 2 * BLOCK] = inner.astype(BF16)
        for tap in range(9):
            small = conv_ref[tap, :, lanes]
            tiled = jnp.concatenate([small] * (BLOCK // group), 0)
            row_shift, col_shift = tap // 3, tap % 3
            taps_ref[row_shift, col_shift * BLOCK : (col_shift + 1) * BLOCK, :] = jnp.where(
                same, tiled, jnp.zeros_like(tiled)
            )
        total = wide_ref[tile_cols : tile_cols + tokens, BLOCK : 2 * BLOCK].astype(F32)
        for row_shift in range(3):
            first = row_shift * tile_cols
            total = total + dot(wide_ref[first : first + tokens, :], taps_ref[row_shift])
        summed_ref[:, lanes] = total

    chunk = 128
    inverse = 1.0 / channels

    def normalise(step, _):
        at = pl.ds(pl.multiple_of(step * chunk, chunk), chunk)
        values = summed_ref[at, :]
        centred = values - jnp.sum(values, axis=-1, keepdims=True) * inverse
        variance = jnp.sum(centred * centred, axis=-1, keepdims=True) * inverse
        features_ref[at, :] = (centred * lax.rsqrt(variance + 1e-05)).astype(BF16)
        return 0

    lax.fori_loop(0, tokens // chunk, normalise, 0)
    store = pltpu.make_async_copy(features_ref, features_hbm, load_sem.at[len(loads)])
    store.start()
    head_dim = channels // heads
    for load in loads[3:]:
        load.wait()

    def ask(step, _):
        at = pl.ds(pl.multiple_of(step * BLOCK, BLOCK), BLOCK)
        asked = dot(latent_ref[...], weight_ref[:, at]).astype(BF16).astype(F32)
        query_ref[:, at] = (asked * head_dim ** -0.5).astype(BF16)
        return 0

    lax.fori_loop(0, channels // BLOCK, ask, 0)

    def project(step, _):
        at = pl.ds(pl.multiple_of(step * BLOCK, BLOCK), BLOCK)
        keys_ref[:, at] = dot(features_ref[...], kv_ref[:, at]).astype(BF16)
        return 0

    lax.fori_loop(0, keys_ref.shape[1] // BLOCK, project, 0)

    latent_count = query_ref.shape[0]
    token_lane = lax.broadcasted_iota(jnp.int32, (tokens, LANES), 1)
    query_lane = lax.broadcasted_iota(jnp.int32, (latent_count, LANES), 1)
    token_low = token_lane < head_dim
    query_low = query_lane < head_dim
    stat_ref[...] = jnp.zeros_like(stat_ref)

    def attend(pair, _):
        at = pl.ds(pl.multiple_of(pair * LANES, LANES), LANES)
        value_at = pl.ds(pl.multiple_of(channels + pair * LANES, LANES), LANES)
        queries = query_ref[:, at]
        keys = keys_ref[:, at]
        values = keys_ref[:, value_at]
        live = live_ref[...]
        bias = (live - 1.0) * (-LOW)
        bias = bias.astype(BF16)
        ones = jnp.ones_like(values)
        results = []
        stats = stat_ref[...]
        for which in range(2):
            query_mine = query_low if which == 0 else jnp.logical_not(query_low)
            token_mine = token_low if which == 0 else jnp.logical_not(token_low)
            spot = head_dim if which == 0 else 0
            marker = (query_lane == spot).astype(F32).astype(BF16)
            query_head = jnp.where(query_mine, queries, marker)
            key_head = jnp.where(token_mine, keys, bias)
            value_head = jnp.where(token_mine, values, ones) * live
            scores = lax.dot_general(
                query_head, key_head, (((1,), (1,)), ((), ())), preferred_element_type=F32
            )
            peak = jnp.max(scores, axis=1, keepdims=True)
            weights = jnp.exp(scores - peak).astype(BF16)
            got = dot(weights, value_head)
            results.append(got)
            head = pair * 2 + which
            total = got[:, spot : spot + 1]
            stats = jnp.where(query_lane == head, peak, stats)
            stats = jnp.where(query_lane == head_dim + head, total, stats)
        stat_ref[...] = stats
        numer = jnp.where(query_low, results[0], results[1])
        denom = jnp.where(query_low, results[1], results[0])
        denom = pltpu.roll(denom, head_dim, 1)
        part_ref[:, at] = jnp.where(denom > 0, numer / jnp.maximum(denom, 1e-30), 0.0).astype(BF16)
        return 0

    lax.fori_loop(0, heads // 2, attend, 0)
    store.wait()


def local_work(borders, live, pixels, patch_weight, conv_weight, latents, query_weight, kv_weight):
    tile_rows, tile_cols, patch_in = pixels.shape
    channels = patch_weight.shape[1]
    tokens = tile_rows * tile_cols
    latent_count = latents.shape[0]
    rows_ext = tile_rows + 2
    vmem = pl.BlockSpec(memory_space=pltpu.VMEM)
    leave = pl.BlockSpec(memory_space=pl.ANY)
    loaded = (
        pixels.reshape(tokens, patch_in), patch_weight, conv_weight, latents, query_weight, kv_weight,
    )
    part, stat, features = pl.pallas_call(
        functools.partial(core, tile_rows, tile_cols, HEADS),
        out_shape=(
            jax.ShapeDtypeStruct((latent_count, channels), BF16),
            jax.ShapeDtypeStruct((latent_count, LANES), F32),
            jax.ShapeDtypeStruct((tokens, channels), BF16),
        ),
        in_specs=[vmem] * 5 + [leave] * len(loaded),
        out_specs=(vmem, vmem, leave),
        scratch_shapes=[pltpu.VMEM(array.shape, BF16) for array in loaded]
        + [
            pltpu.VMEM((rows_ext * tile_cols, 3 * BLOCK), BF16),
            pltpu.VMEM((3, 3 * BLOCK, BLOCK), BF16),
            pltpu.VMEM((tokens, channels), F32),
            pltpu.VMEM((tokens, 2 * channels), BF16),
            pltpu.VMEM((latent_count, channels), BF16),
            pltpu.VMEM((tokens, channels), BF16),
            pltpu.SemaphoreType.DMA((len(loaded) + 1,)),
        ],
        compiler_params=pltpu.CompilerParams(vmem_limit_bytes=60 * 1024 * 1024),
        name="local_work",
    )(*borders, live, *loaded)
    return features, part, stat


def greet(
    pixels_ref, first_ref, last_ref,
    top_ref, bottom_ref, left_ref, right_ref,
    send_sem, recv_sem,
):
    tile_rows, tile_cols, _ = pixels_ref.shape
    row_count, col_count = lax.axis_size("rows"), lax.axis_size("cols")
    row, col = lax.axis_index("rows"), lax.axis_index("cols")
    low, high = slice(0, CORNER), slice(tile_cols - CORNER, tile_cols)
    column = slice(0, tile_rows)
    above = slice(tile_rows, tile_rows + CORNER)
    below = slice(tile_rows + CORNER, tile_rows + 2 * CORNER)
    end = tile_rows - 1
    moves = (
        (1, 0, pixels_ref.at[end], top_ref),
        (-1, 0, pixels_ref.at[0], bottom_ref),
        (0, 1, last_ref, left_ref.at[column]),
        (0, -1, first_ref, right_ref.at[column]),
        (1, 1, pixels_ref.at[end, high], left_ref.at[above]),
        (1, -1, pixels_ref.at[end, low], right_ref.at[above]),
        (-1, 1, pixels_ref.at[0, high], left_ref.at[below]),
        (-1, -1, pixels_ref.at[0, low], right_ref.at[below]),
    )

    def inside(down, across):
        ok = None
        for at, step, count in ((row, down, row_count), (col, across, col_count)):
            if step:
                here = at + step < count if step > 0 else at + step >= 0
                ok = here if ok is None else jnp.logical_and(ok, here)
        return ok

    barrier = pltpu.get_barrier_semaphore()
    for down, across, _, _ in moves:
        @pl.when(inside(down, across))
        def _(down=down, across=across):
            pl.semaphore_signal(
                barrier, inc=1, device_id=(row + down, col + across), device_id_type=MESH
            )
    tall = 1 + (row > 0).astype(jnp.int32) + (row < row_count - 1).astype(jnp.int32)
    wide = 1 + (col > 0).astype(jnp.int32) + (col < col_count - 1).astype(jnp.int32)
    pl.semaphore_wait(barrier, tall * wide - 1)

    def make(number):
        down, across, source, target = moves[number]
        return pltpu.make_async_remote_copy(
            src_ref=source, dst_ref=target,
            send_sem=send_sem.at[number], recv_sem=recv_sem.at[number],
            device_id=(row + down, col + across), device_id_type=MESH,
        )

    for number, (down, across, _, _) in enumerate(moves):
        @pl.when(inside(down, across))
        def _(number=number):
            make(number).start()
    for number, (down, across, _, target) in enumerate(moves):
        @pl.when(inside(-down, -across))
        def _(number=number):
            make(number).wait_recv()

        @pl.when(jnp.logical_not(inside(-down, -across)))
        def _(target=target):
            target[...] = jnp.zeros(target.shape, BF16)
    for number, (down, across, _, _) in enumerate(moves):
        @pl.when(inside(down, across))
        def _(number=number):
            make(number).wait_send()


def borders_of(pixels):
    tile_rows, tile_cols, patch_in = pixels.shape
    vmem = pl.BlockSpec(memory_space=pltpu.VMEM)
    flat = jax.ShapeDtypeStruct((tile_cols, patch_in), BF16)
    tall = jax.ShapeDtypeStruct((tile_rows + 2 * CORNER, patch_in), BF16)
    return pl.pallas_call(
        greet,
        out_shape=(flat, flat, tall, tall),
        in_specs=[pl.BlockSpec(memory_space=pl.ANY), vmem, vmem],
        out_specs=(vmem,) * 4,
        scratch_shapes=[pltpu.SemaphoreType.DMA((8,)), pltpu.SemaphoreType.DMA((8,))],
        compiler_params=pltpu.CompilerParams(
            collective_id=2, has_side_effects=True, vmem_limit_bytes=60 * 1024 * 1024
        ),
        name="borders",
    )(pixels, pixels[:, 0], pixels[:, -1])


def spread(values, heads, head_dim, low):
    return [
        jnp.where(low, values[:, 2 * pair : 2 * pair + 1], values[:, 2 * pair + 1 : 2 * pair + 2])
        for pair in range(heads // 2)
    ]


def blend(parts, stats, heads, head_dim):
    rows = parts[0].shape[0]
    lane = lax.broadcasted_iota(jnp.int32, (rows, LANES), 1)
    low = lane < head_dim
    peaks = stats
    totals = [pltpu.roll(stat, LANES - head_dim, 1) for stat in stats]
    top = functools.reduce(jnp.maximum, peaks)
    shares = [jnp.exp(peak - top) * total for peak, total in zip(peaks, totals)]
    whole = functools.reduce(jnp.add, shares)
    inverse = jnp.where(whole > 0, 1.0 / jnp.maximum(whole, 1e-30), 0.0)
    columns = [0.0] * (heads // 2)
    for part, share in zip(parts, shares):
        factors = spread(share * inverse, heads, head_dim, low)
        for pair in range(heads // 2):
            piece = part[:, pair * LANES : (pair + 1) * LANES].astype(F32)
            columns[pair] = columns[pair] + factors[pair] * piece
    used = lane < heads
    stat = jnp.where(used, top, 0.0)
    stat = jnp.where(lane < head_dim, stat, pltpu.roll(jnp.where(used, whole, 0.0), head_dim, 1))
    return columns, stat


def exchange(
    heads,
    part_ref, stat_ref, weight_hbm,
    out_ref,
    part_one, stat_one, sum_one, tot_one, part_two, stat_two, sum_two, tot_two,
    part_three, stat_three, weight_ref, send_sem, recv_sem, load_sem,
):
    row_count, half, _, own, channels = part_ref.shape
    head_dim = channels // heads
    row = lax.axis_index("rows")
    col = lax.axis_index("cols")
    side = lax.rem(col, 2)
    slot = lax.div(col, 2)
    load = pltpu.make_async_copy(weight_hbm, weight_ref, load_sem)
    load.start()

    twin = (row, slot * 2 + (1 - side))
    row_peers = [(lax.rem(row + step, row_count), col) for step in range(1, row_count)]
    col_peers = [(row, lax.rem(slot + step, half) * 2 + side) for step in range(1, half)]
    barrier = pltpu.get_barrier_semaphore()
    for peer in [twin] + row_peers + col_peers:
        pl.semaphore_signal(barrier, inc=1, device_id=peer, device_id_type=MESH)
    pl.semaphore_wait(barrier, 1 + len(row_peers) + len(col_peers))

    def send(source, target, peer, number):
        copy = pltpu.make_async_remote_copy(
            src_ref=source, dst_ref=target,
            send_sem=send_sem.at[number], recv_sem=recv_sem.at[number],
            device_id=peer, device_id_type=MESH,
        )
        copy.start()
        return copy

    copies = [
        send(part_ref.at[:, :, 1 - side], part_one, twin, 0),
        send(stat_ref.at[:, :, 1 - side], stat_one, twin, 1),
    ]
    for copy in copies:
        copy.wait()

    def first(index, _):
        a, b = lax.div(index, half), lax.rem(index, half)
        columns, stat = blend(
            [part_ref[a, b, side], part_one[a, b]], [stat_ref[a, b, side], stat_one[a, b]],
            heads, head_dim,
        )
        for pair, column in enumerate(columns):
            sum_one[a, b, :, pair * LANES : (pair + 1) * LANES] = column.astype(BF16)
        tot_one[a, b] = stat
        return 0

    lax.fori_loop(0, row_count * half, first, 0)

    copies = []
    for step, peer in enumerate(row_peers):
        number = 2 + 2 * step
        copies.append(send(sum_one.at[peer[0]], part_two.at[step], peer, number))
        copies.append(send(tot_one.at[peer[0]], stat_two.at[step], peer, number + 1))
    for copy in copies:
        copy.wait()

    def second(b, _):
        columns, stat = blend(
            [sum_one[row, b]] + [part_two[step, b] for step in range(row_count - 1)],
            [tot_one[row, b]] + [stat_two[step, b] for step in range(row_count - 1)],
            heads, head_dim,
        )
        for pair, column in enumerate(columns):
            sum_two[b, :, pair * LANES : (pair + 1) * LANES] = column.astype(BF16)
        tot_two[b] = stat
        return 0

    lax.fori_loop(0, half, second, 0)

    copies = []
    for step, peer in enumerate(col_peers):
        number = 2 * row_count + 2 * step
        where = lax.rem(slot + step + 1, half)
        copies.append(send(sum_two.at[where], part_three.at[step], peer, number))
        copies.append(send(tot_two.at[where], stat_three.at[step], peer, number + 1))
    for copy in copies:
        copy.wait()
    columns, _ = blend(
        [sum_two[slot]] + [part_three[step] for step in range(half - 1)],
        [tot_two[slot]] + [stat_three[step] for step in range(half - 1)],
        heads, head_dim,
    )
    attended = jnp.concatenate(columns, 1)
    mean = jnp.sum(attended * attended, axis=-1, keepdims=True) * (1.0 / channels)
    normed = (attended * lax.rsqrt(mean + 1e-06)).astype(BF16)
    load.wait()
    out_ref[...] = dot(normed, weight_ref[...]).astype(BF16)


def combine(part, stat, out_weight):
    row_count, col_count = lax.axis_size("rows"), lax.axis_size("cols")
    half = col_count // 2
    latent_count, channels = part.shape
    own = latent_count // (row_count * col_count)
    part = part.reshape(row_count, half, 2, own, channels)
    stat = stat.reshape(row_count, half, 2, own, LANES)
    vmem = pl.BlockSpec(memory_space=pltpu.VMEM)
    copies = 2 + 2 * (row_count - 1) + 2 * (half - 1)

    def pairs(*extent):
        return [
            pltpu.VMEM(extent + (own, channels), BF16), pltpu.VMEM(extent + (own, LANES), F32)
        ]

    return pl.pallas_call(
        functools.partial(exchange, HEADS),
        out_shape=jax.ShapeDtypeStruct((own, out_weight.shape[1]), BF16),
        in_specs=[vmem, vmem, pl.BlockSpec(memory_space=pl.ANY)],
        out_specs=vmem,
        scratch_shapes=pairs(row_count, half)
        + pairs(row_count, half)
        + pairs(row_count - 1, half)
        + pairs(half)
        + pairs(half - 1)
        + [
            pltpu.VMEM(out_weight.shape, BF16),
            pltpu.SemaphoreType.DMA((copies,)),
            pltpu.SemaphoreType.DMA((copies,)),
            pltpu.SemaphoreType.DMA,
        ],
        compiler_params=pltpu.CompilerParams(
            collective_id=1, has_side_effects=True, vmem_limit_bytes=24 * 1024 * 1024
        ),
        name="combine",
    )(part, stat, out_weight)


def shards(pixels, tissue, patch_weight, conv_weight, kv_weight, query_weight, out_weight, latents):
    tile_rows, tile_cols, _ = pixels.shape
    channels = patch_weight.shape[1]
    tokens = tile_rows * tile_cols
    live = jnp.broadcast_to((tissue.reshape(tokens, 1) > 0).astype(BF16), (tokens, LANES))
    features, part, stat = local_work(
        borders_of(pixels), live, pixels, patch_weight, conv_weight, latents, query_weight, kv_weight
    )
    latents_out = combine(part, stat, out_weight)
    return (features.reshape(tile_rows, tile_cols, channels), latents_out)


def solution(mesh):
    return jax.shard_map(
        shards,
        mesh=mesh,
        in_specs=(P("rows", "cols", None), P("rows", "cols"), P(), P(), P(), P(), P(), P()),
        out_specs=(P("rows", "cols", None), P(("rows", "cols"), None)),
        check_vma=False,
    )
```

```python
import functools

import jax
import jax.numpy as jnp
from jax import lax
from jax.experimental import pallas as pl
from jax.experimental.pallas import tpu as pltpu
from jax.sharding import PartitionSpec as P

HEADS = 16
BLOCK = 256
LANES = 128
PAD = 8
CORNER = 16
F32 = jnp.float32
BF16 = jnp.bfloat16
LOW = -1e30
MESH = pl.DeviceIdType.MESH


def dot(a, b):
    return jnp.dot(a, b, preferred_element_type=F32)


def core(
    tile_rows, tile_cols, heads,
    top_ref, bottom_ref, left_ref, right_ref, live_ref,
    main_hbm, patch_hbm, conv_hbm, query_hbm, kv_hbm,
    part_ref, stat_ref, features_hbm,
    main_ref, patch_ref, conv_ref, query_ref, kv_ref,
    wide_ref, taps_ref, summed_ref, keys_ref, features_ref, load_sem,
):
    loads = [
        pltpu.make_async_copy(source, target, load_sem.at[number])
        for number, (source, target) in enumerate(
            (
                (main_hbm, main_ref), (patch_hbm, patch_ref), (conv_hbm, conv_ref),
                (query_hbm, query_ref), (kv_hbm, kv_ref),
            )
        )
    ]
    for load in loads:
        load.start()
    tokens = tile_rows * tile_cols
    channels = patch_ref.shape[1]
    group = conv_ref.shape[1]
    rows_ext = tile_rows + 2
    col_ext = tile_cols + PAD
    same = (
        lax.broadcasted_iota(jnp.int32, (BLOCK, BLOCK), 0) // group
        == lax.broadcasted_iota(jnp.int32, (BLOCK, BLOCK), 1) // group
    )
    side_slot = lax.broadcasted_iota(jnp.int32, (rows_ext, PAD, BLOCK), 1)
    tall = (1, PAD, BLOCK)

    def border(values, upper, lower):
        return (
            jnp.broadcast_to(values[upper : upper + 1][:, None, :], tall),
            jnp.broadcast_to(values[:tile_rows][:, None, :], (tile_rows, PAD, BLOCK)),
            jnp.broadcast_to(values[lower : lower + 1][:, None, :], tall),
        )

    for load in loads[:3]:
        load.wait()
    for block in range(channels // BLOCK):
        lanes = slice(block * BLOCK, (block + 1) * BLOCK)
        patch = patch_ref[:, lanes]
        inner = jnp.concatenate(
            [dot(top_ref[...], patch), dot(main_ref[...], patch), dot(bottom_ref[...], patch)], 0
        )
        upper, middle, lower = border(
            dot(left_ref[...], patch), tile_rows + CORNER - 1, tile_rows + 2 * CORNER - 1
        )
        from_left = jnp.concatenate([middle, lower, upper], 0)
        upper, middle, lower = border(
            dot(right_ref[...], patch), tile_rows, tile_rows + CORNER
        )
        from_right = jnp.concatenate([upper, middle, lower], 0)
        side = jnp.where(side_slot == PAD - 1, from_left, from_right)
        full = jnp.concatenate(
            [inner.reshape(rows_ext, tile_cols, BLOCK), side], 1
        ).reshape(rows_ext * col_ext, BLOCK)
        for col_shift, amount in ((0, 1), (2, rows_ext * col_ext - 1)):
            moved = pltpu.roll(full, amount, 0).reshape(rows_ext, col_ext, BLOCK)
            moved = moved[:, :tile_cols].reshape(rows_ext * tile_cols, BLOCK)
            wide_ref[:, col_shift * BLOCK : (col_shift + 1) * BLOCK] = moved.astype(BF16)
        wide_ref[:, BLOCK : 2 * BLOCK] = inner.astype(BF16)
        for tap in range(9):
            small = conv_ref[tap, :, lanes]
            tiled = jnp.concatenate([small] * (BLOCK // group), 0)
            row_shift, col_shift = tap // 3, tap % 3
            taps_ref[row_shift, col_shift * BLOCK : (col_shift + 1) * BLOCK, :] = jnp.where(
                same, tiled, jnp.zeros_like(tiled)
            )
        total = wide_ref[tile_cols : tile_cols + tokens, BLOCK : 2 * BLOCK].astype(F32)
        for row_shift in range(3):
            first = row_shift * tile_cols
            total = total + dot(wide_ref[first : first + tokens, :], taps_ref[row_shift])
        summed_ref[:, lanes] = total

    chunk = 128
    inverse = 1.0 / channels

    def normalise(step, _):
        at = pl.ds(pl.multiple_of(step * chunk, chunk), chunk)
        values = summed_ref[at, :]
        centred = values - jnp.sum(values, axis=-1, keepdims=True) * inverse
        variance = jnp.sum(centred * centred, axis=-1, keepdims=True) * inverse
        features_ref[at, :] = (centred * lax.rsqrt(variance + 1e-05)).astype(BF16)
        return 0

    lax.fori_loop(0, tokens // chunk, normalise, 0)
    store = pltpu.make_async_copy(features_ref, features_hbm, load_sem.at[len(loads)])
    store.start()
    head_dim = channels // heads
    for load in loads[3:]:
        load.wait()

    def project(step, _):
        at = pl.ds(pl.multiple_of(step * BLOCK, BLOCK), BLOCK)
        keys_ref[:, at] = dot(features_ref[...], kv_ref[:, at]).astype(BF16)
        return 0

    lax.fori_loop(0, keys_ref.shape[1] // BLOCK, project, 0)

    latent_count = query_ref.shape[0]
    token_lane = lax.broadcasted_iota(jnp.int32, (tokens, LANES), 1)
    query_lane = lax.broadcasted_iota(jnp.int32, (latent_count, LANES), 1)
    token_low = token_lane < head_dim
    query_low = query_lane < head_dim
    stat_ref[...] = jnp.zeros_like(stat_ref)

    def attend(pair, _):
        at = pl.ds(pl.multiple_of(pair * LANES, LANES), LANES)
        value_at = pl.ds(pl.multiple_of(channels + pair * LANES, LANES), LANES)
        queries = query_ref[:, at]
        keys = keys_ref[:, at]
        values = keys_ref[:, value_at]
        live = live_ref[...]
        bias = (live - 1.0) * (-LOW)
        bias = bias.astype(BF16)
        ones = jnp.ones_like(values)
        results = []
        stats = stat_ref[...]
        for which in range(2):
            query_mine = query_low if which == 0 else jnp.logical_not(query_low)
            token_mine = token_low if which == 0 else jnp.logical_not(token_low)
            spot = head_dim if which == 0 else 0
            marker = (query_lane == spot).astype(F32).astype(BF16)
            query_head = jnp.where(query_mine, queries, marker)
            key_head = jnp.where(token_mine, keys, bias)
            value_head = jnp.where(token_mine, values, ones) * live
            scores = lax.dot_general(
                query_head, key_head, (((1,), (1,)), ((), ())), preferred_element_type=F32
            )
            peak = jnp.max(scores, axis=1, keepdims=True)
            weights = jnp.exp(scores - peak).astype(BF16)
            got = dot(weights, value_head)
            results.append(got)
            head = pair * 2 + which
            total = got[:, spot : spot + 1]
            stats = jnp.where(query_lane == head, peak, stats)
            stats = jnp.where(query_lane == head_dim + head, total, stats)
        stat_ref[...] = stats
        numer = jnp.where(query_low, results[0], results[1])
        denom = jnp.where(query_low, results[1], results[0])
        denom = pltpu.roll(denom, head_dim, 1)
        part_ref[:, at] = jnp.where(denom > 0, numer / jnp.maximum(denom, 1e-30), 0.0).astype(BF16)
        return 0

    lax.fori_loop(0, heads // 2, attend, 0)
    store.wait()


def local_work(borders, queries, live, pixels, patch_weight, conv_weight, kv_weight):
    tile_rows, tile_cols, patch_in = pixels.shape
    channels = patch_weight.shape[1]
    tokens = tile_rows * tile_cols
    latent_count = queries.shape[0]
    rows_ext = tile_rows + 2
    vmem = pl.BlockSpec(memory_space=pltpu.VMEM)
    leave = pl.BlockSpec(memory_space=pl.ANY)
    loaded = (
        pixels.reshape(tokens, patch_in), patch_weight, conv_weight, queries, kv_weight,
    )
    part, stat, features = pl.pallas_call(
        functools.partial(core, tile_rows, tile_cols, HEADS),
        out_shape=(
            jax.ShapeDtypeStruct((latent_count, channels), BF16),
            jax.ShapeDtypeStruct((latent_count, LANES), F32),
            jax.ShapeDtypeStruct((tokens, channels), BF16),
        ),
        in_specs=[vmem] * 5 + [leave] * len(loaded),
        out_specs=(vmem, vmem, leave),
        scratch_shapes=[pltpu.VMEM(array.shape, BF16) for array in loaded]
        + [
            pltpu.VMEM((rows_ext * tile_cols, 3 * BLOCK), BF16),
            pltpu.VMEM((3, 3 * BLOCK, BLOCK), BF16),
            pltpu.VMEM((tokens, channels), F32),
            pltpu.VMEM((tokens, 2 * channels), BF16),
            pltpu.VMEM((tokens, channels), BF16),
            pltpu.SemaphoreType.DMA((len(loaded) + 1,)),
        ],
        compiler_params=pltpu.CompilerParams(vmem_limit_bytes=60 * 1024 * 1024),
        name="local_work",
    )(*borders, live, *loaded)
    return features, part, stat


def greet(
    head_dim,
    pixels_ref, first_ref, last_ref, latent_hbm, weight_hbm,
    top_ref, bottom_ref, left_ref, right_ref, query_ref,
    latent_ref, weight_ref, send_sem, recv_sem, load_sem,
):
    loads = [
        pltpu.make_async_copy(latent_hbm, latent_ref, load_sem.at[0]),
        pltpu.make_async_copy(weight_hbm, weight_ref, load_sem.at[1]),
    ]
    for load in loads:
        load.start()
    channels = query_ref.shape[1]
    tile_rows, tile_cols, _ = pixels_ref.shape
    row_count, col_count = lax.axis_size("rows"), lax.axis_size("cols")
    row, col = lax.axis_index("rows"), lax.axis_index("cols")
    low, high = slice(0, CORNER), slice(tile_cols - CORNER, tile_cols)
    column = slice(0, tile_rows)
    above = slice(tile_rows, tile_rows + CORNER)
    below = slice(tile_rows + CORNER, tile_rows + 2 * CORNER)
    end = tile_rows - 1
    moves = (
        (1, 0, pixels_ref.at[end], top_ref),
        (-1, 0, pixels_ref.at[0], bottom_ref),
        (0, 1, last_ref, left_ref.at[column]),
        (0, -1, first_ref, right_ref.at[column]),
        (1, 1, pixels_ref.at[end, high], left_ref.at[above]),
        (1, -1, pixels_ref.at[end, low], right_ref.at[above]),
        (-1, 1, pixels_ref.at[0, high], left_ref.at[below]),
        (-1, -1, pixels_ref.at[0, low], right_ref.at[below]),
    )

    def inside(down, across):
        ok = None
        for at, step, count in ((row, down, row_count), (col, across, col_count)):
            if step:
                here = at + step < count if step > 0 else at + step >= 0
                ok = here if ok is None else jnp.logical_and(ok, here)
        return ok

    barrier = pltpu.get_barrier_semaphore()
    for down, across, _, _ in moves:
        @pl.when(inside(down, across))
        def _(down=down, across=across):
            pl.semaphore_signal(
                barrier, inc=1, device_id=(row + down, col + across), device_id_type=MESH
            )
    tall = 1 + (row > 0).astype(jnp.int32) + (row < row_count - 1).astype(jnp.int32)
    wide = 1 + (col > 0).astype(jnp.int32) + (col < col_count - 1).astype(jnp.int32)
    pl.semaphore_wait(barrier, tall * wide - 1)

    def make(number):
        down, across, source, target = moves[number]
        return pltpu.make_async_remote_copy(
            src_ref=source, dst_ref=target,
            send_sem=send_sem.at[number], recv_sem=recv_sem.at[number],
            device_id=(row + down, col + across), device_id_type=MESH,
        )

    for number, (down, across, _, _) in enumerate(moves):
        @pl.when(inside(down, across))
        def _(number=number):
            make(number).start()
    for load in loads:
        load.wait()

    def ask(step, _):
        at = pl.ds(pl.multiple_of(step * BLOCK, BLOCK), BLOCK)
        asked = dot(latent_ref[...], weight_ref[:, at]).astype(BF16).astype(F32)
        query_ref[:, at] = (asked * head_dim ** -0.5).astype(BF16)
        return 0

    lax.fori_loop(0, channels // BLOCK, ask, 0)
    for number, (down, across, _, target) in enumerate(moves):
        @pl.when(inside(-down, -across))
        def _(number=number):
            make(number).wait_recv()

        @pl.when(jnp.logical_not(inside(-down, -across)))
        def _(target=target):
            target[...] = jnp.zeros(target.shape, BF16)
    for number, (down, across, _, _) in enumerate(moves):
        @pl.when(inside(down, across))
        def _(number=number):
            make(number).wait_send()


def borders_of(pixels, latents, query_weight):
    tile_rows, tile_cols, patch_in = pixels.shape
    vmem = pl.BlockSpec(memory_space=pltpu.VMEM)
    flat = jax.ShapeDtypeStruct((tile_cols, patch_in), BF16)
    tall = jax.ShapeDtypeStruct((tile_rows + 2 * CORNER, patch_in), BF16)
    channels = query_weight.shape[1]
    leave = pl.BlockSpec(memory_space=pl.ANY)
    *borders, queries = pl.pallas_call(
        functools.partial(greet, channels // HEADS),
        out_shape=(flat, flat, tall, tall, jax.ShapeDtypeStruct((latents.shape[0], channels), BF16)),
        in_specs=[leave, vmem, vmem, leave, leave],
        out_specs=(vmem,) * 5,
        scratch_shapes=[
            pltpu.VMEM(latents.shape, BF16),
            pltpu.VMEM(query_weight.shape, BF16),
            pltpu.SemaphoreType.DMA((8,)),
            pltpu.SemaphoreType.DMA((8,)),
            pltpu.SemaphoreType.DMA((2,)),
        ],
        compiler_params=pltpu.CompilerParams(
            collective_id=2, has_side_effects=True, vmem_limit_bytes=60 * 1024 * 1024
        ),
        name="borders",
    )(pixels, pixels[:, 0], pixels[:, -1], latents, query_weight)
    return borders, queries


def spread(values, heads, head_dim, low):
    return [
        jnp.where(low, values[:, 2 * pair : 2 * pair + 1], values[:, 2 * pair + 1 : 2 * pair + 2])
        for pair in range(heads // 2)
    ]


def blend(parts, stats, heads, head_dim):
    rows = parts[0].shape[0]
    lane = lax.broadcasted_iota(jnp.int32, (rows, LANES), 1)
    low = lane < head_dim
    peaks = stats
    totals = [pltpu.roll(stat, LANES - head_dim, 1) for stat in stats]
    top = functools.reduce(jnp.maximum, peaks)
    shares = [jnp.exp(peak - top) * total for peak, total in zip(peaks, totals)]
    whole = functools.reduce(jnp.add, shares)
    inverse = jnp.where(whole > 0, 1.0 / jnp.maximum(whole, 1e-30), 0.0)
    columns = [0.0] * (heads // 2)
    for part, share in zip(parts, shares):
        factors = spread(share * inverse, heads, head_dim, low)
        for pair in range(heads // 2):
            piece = part[:, pair * LANES : (pair + 1) * LANES].astype(F32)
            columns[pair] = columns[pair] + factors[pair] * piece
    used = lane < heads
    stat = jnp.where(used, top, 0.0)
    stat = jnp.where(lane < head_dim, stat, pltpu.roll(jnp.where(used, whole, 0.0), head_dim, 1))
    return columns, stat


def exchange(
    heads,
    part_ref, stat_ref, weight_hbm,
    out_ref,
    part_one, stat_one, sum_one, tot_one, part_two, stat_two, sum_two, tot_two,
    part_three, stat_three, weight_ref, send_sem, recv_sem, load_sem,
):
    row_count, half, _, own, channels = part_ref.shape
    head_dim = channels // heads
    row = lax.axis_index("rows")
    col = lax.axis_index("cols")
    side = lax.rem(col, 2)
    slot = lax.div(col, 2)
    load = pltpu.make_async_copy(weight_hbm, weight_ref, load_sem)
    load.start()

    twin = (row, slot * 2 + (1 - side))
    row_peers = [(lax.rem(row + step, row_count), col) for step in range(1, row_count)]
    col_peers = [(row, lax.rem(slot + step, half) * 2 + side) for step in range(1, half)]
    barrier = pltpu.get_barrier_semaphore()
    for peer in [twin] + row_peers + col_peers:
        pl.semaphore_signal(barrier, inc=1, device_id=peer, device_id_type=MESH)
    pl.semaphore_wait(barrier, 1 + len(row_peers) + len(col_peers))

    def send(source, target, peer, number):
        copy = pltpu.make_async_remote_copy(
            src_ref=source, dst_ref=target,
            send_sem=send_sem.at[number], recv_sem=recv_sem.at[number],
            device_id=peer, device_id_type=MESH,
        )
        copy.start()
        return copy

    row_order = [lax.rem(row + step, row_count) for step in range(1, row_count + 1)]
    col_order = [lax.rem(slot + step, half) for step in range(1, half + 1)]
    ones, twos, threes = [], [], []
    for step, a in enumerate(row_order):
        ones.append(
            (
                send(part_ref.at[a, :, 1 - side], part_one.at[a], twin, 2 * step),
                send(stat_ref.at[a, :, 1 - side], stat_one.at[a], twin, 2 * step + 1),
            )
        )
    number = 2 * row_count
    for step, a in enumerate(row_order):
        for copy in ones[step]:
            copy.wait_recv()

        def first(b, _, a=a):
            columns, stat = blend(
                [part_ref[a, b, side], part_one[a, b]], [stat_ref[a, b, side], stat_one[a, b]],
                heads, head_dim,
            )
            for pair, column in enumerate(columns):
                sum_one[a, b, :, pair * LANES : (pair + 1) * LANES] = column.astype(BF16)
            tot_one[a, b] = stat
            return 0

        lax.fori_loop(0, half, first, 0)
        if step < row_count - 1:
            twos.append(send(sum_one.at[a], part_two.at[step], row_peers[step], number))
            twos.append(send(tot_one.at[a], stat_two.at[step], row_peers[step], number + 1))
            number += 2
    for copy in twos:
        copy.wait_recv()
    for step, b in enumerate(col_order):
        columns, stat = blend(
            [sum_one[row, b]] + [part_two[other, b] for other in range(row_count - 1)],
            [tot_one[row, b]] + [stat_two[other, b] for other in range(row_count - 1)],
            heads, head_dim,
        )
        if step < half - 1:
            for pair, column in enumerate(columns):
                sum_two[b, :, pair * LANES : (pair + 1) * LANES] = column.astype(BF16)
            tot_two[b] = stat
            threes.append(send(sum_two.at[b], part_three.at[step], col_peers[step], number))
            threes.append(send(tot_two.at[b], stat_three.at[step], col_peers[step], number + 1))
            number += 2
    for copy in threes:
        copy.wait_recv()
    columns, _ = blend(
        [jnp.concatenate(columns, 1)] + [part_three[step] for step in range(half - 1)],
        [stat] + [stat_three[step] for step in range(half - 1)],
        heads, head_dim,
    )
    for copy in [copy for both in ones for copy in both] + twos + threes:
        copy.wait_send()
    attended = jnp.concatenate(columns, 1)
    mean = jnp.sum(attended * attended, axis=-1, keepdims=True) * (1.0 / channels)
    normed = (attended * lax.rsqrt(mean + 1e-06)).astype(BF16)
    load.wait()
    out_ref[...] = dot(normed, weight_ref[...]).astype(BF16)


def combine(part, stat, out_weight):
    row_count, col_count = lax.axis_size("rows"), lax.axis_size("cols")
    half = col_count // 2
    latent_count, channels = part.shape
    own = latent_count // (row_count * col_count)
    part = part.reshape(row_count, half, 2, own, channels)
    stat = stat.reshape(row_count, half, 2, own, LANES)
    vmem = pl.BlockSpec(memory_space=pltpu.VMEM)
    copies = 2 * (2 * row_count - 1) + 2 * (half - 1)

    def pairs(*extent):
        return [
            pltpu.VMEM(extent + (own, channels), BF16), pltpu.VMEM(extent + (own, LANES), F32)
        ]

    return pl.pallas_call(
        functools.partial(exchange, HEADS),
        out_shape=jax.ShapeDtypeStruct((own, out_weight.shape[1]), BF16),
        in_specs=[vmem, vmem, pl.BlockSpec(memory_space=pl.ANY)],
        out_specs=vmem,
        scratch_shapes=pairs(row_count, half)
        + pairs(row_count, half)
        + pairs(row_count - 1, half)
        + pairs(half)
        + pairs(half - 1)
        + [
            pltpu.VMEM(out_weight.shape, BF16),
            pltpu.SemaphoreType.DMA((copies,)),
            pltpu.SemaphoreType.DMA((copies,)),
            pltpu.SemaphoreType.DMA,
        ],
        compiler_params=pltpu.CompilerParams(
            collective_id=1, has_side_effects=True, vmem_limit_bytes=24 * 1024 * 1024
        ),
        name="combine",
    )(part, stat, out_weight)


def shards(pixels, tissue, patch_weight, conv_weight, kv_weight, query_weight, out_weight, latents):
    tile_rows, tile_cols, _ = pixels.shape
    channels = patch_weight.shape[1]
    tokens = tile_rows * tile_cols
    live = jnp.broadcast_to((tissue.reshape(tokens, 1) > 0).astype(BF16), (tokens, LANES))
    borders, queries = borders_of(pixels, latents, query_weight)
    features, part, stat = local_work(
        borders, queries, live, pixels, patch_weight, conv_weight, kv_weight
    )
    latents_out = combine(part, stat, out_weight)
    return (features.reshape(tile_rows, tile_cols, channels), latents_out)


def solution(mesh):
    return jax.shard_map(
        shards,
        mesh=mesh,
        in_specs=(P("rows", "cols", None), P("rows", "cols"), P(), P(), P(), P(), P(), P()),
        out_specs=(P("rows", "cols", None), P(("rows", "cols"), None)),
        check_vma=False,
    )
```

```python
import functools

import jax
import jax.numpy as jnp
from jax import lax
from jax.experimental import pallas as pl
from jax.experimental.pallas import tpu as pltpu
from jax.sharding import PartitionSpec as P

HEADS = 16
BLOCK = 256
LANES = 128
PAD = 8
CORNER = 16
F32 = jnp.float32
BF16 = jnp.bfloat16
LOW = -1e30
MESH = pl.DeviceIdType.MESH


def dot(a, b):
    return jnp.dot(a, b, preferred_element_type=F32)


def core(
    tile_rows, tile_cols, heads,
    top_ref, bottom_ref, left_ref, right_ref, live_ref,
    main_hbm, patch_hbm, conv_hbm, query_hbm, kv_hbm,
    part_ref, stat_ref, features_hbm,
    main_ref, patch_ref, conv_ref, query_ref, kv_ref,
    wide_ref, taps_ref, summed_ref, keys_ref, features_ref, load_sem,
):
    loads = [
        pltpu.make_async_copy(source, target, load_sem.at[number])
        for number, (source, target) in enumerate(
            (
                (main_hbm, main_ref), (patch_hbm, patch_ref), (conv_hbm, conv_ref),
                (query_hbm, query_ref), (kv_hbm, kv_ref),
            )
        )
    ]
    for load in loads:
        load.start()
    tokens = tile_rows * tile_cols
    channels = patch_ref.shape[1]
    group = conv_ref.shape[1]
    rows_ext = tile_rows + 2
    col_ext = tile_cols + PAD
    same = (
        lax.broadcasted_iota(jnp.int32, (BLOCK, BLOCK), 0) // group
        == lax.broadcasted_iota(jnp.int32, (BLOCK, BLOCK), 1) // group
    )
    side_slot = lax.broadcasted_iota(jnp.int32, (rows_ext, PAD, BLOCK), 1)
    tall = (1, PAD, BLOCK)

    def border(values, upper, lower):
        return (
            jnp.broadcast_to(values[upper : upper + 1][:, None, :], tall),
            jnp.broadcast_to(values[:tile_rows][:, None, :], (tile_rows, PAD, BLOCK)),
            jnp.broadcast_to(values[lower : lower + 1][:, None, :], tall),
        )

    for load in loads[:3]:
        load.wait()
    for block in range(channels // BLOCK):
        lanes = slice(block * BLOCK, (block + 1) * BLOCK)
        patch = patch_ref[:, lanes]
        inner = jnp.concatenate(
            [dot(top_ref[...], patch), dot(main_ref[...], patch), dot(bottom_ref[...], patch)], 0
        )
        upper, middle, lower = border(
            dot(left_ref[...], patch), tile_rows + CORNER - 1, tile_rows + 2 * CORNER - 1
        )
        from_left = jnp.concatenate([middle, lower, upper], 0)
        upper, middle, lower = border(
            dot(right_ref[...], patch), tile_rows, tile_rows + CORNER
        )
        from_right = jnp.concatenate([upper, middle, lower], 0)
        side = jnp.where(side_slot == PAD - 1, from_left, from_right)
        full = jnp.concatenate(
            [inner.reshape(rows_ext, tile_cols, BLOCK), side], 1
        ).reshape(rows_ext * col_ext, BLOCK)
        for col_shift, amount in ((0, 1), (2, rows_ext * col_ext - 1)):
            moved = pltpu.roll(full, amount, 0).reshape(rows_ext, col_ext, BLOCK)
            moved = moved[:, :tile_cols].reshape(rows_ext * tile_cols, BLOCK)
            wide_ref[:, col_shift * BLOCK : (col_shift + 1) * BLOCK] = moved.astype(BF16)
        wide_ref[:, BLOCK : 2 * BLOCK] = inner.astype(BF16)
        for tap in range(9):
            small = conv_ref[tap, :, lanes]
            tiled = jnp.concatenate([small] * (BLOCK // group), 0)
            row_shift, col_shift = tap // 3, tap % 3
            taps_ref[row_shift, col_shift * BLOCK : (col_shift + 1) * BLOCK, :] = jnp.where(
                same, tiled, jnp.zeros_like(tiled)
            )
        total = wide_ref[tile_cols : tile_cols + tokens, BLOCK : 2 * BLOCK].astype(F32)
        for row_shift in range(3):
            first = row_shift * tile_cols
            total = total + dot(wide_ref[first : first + tokens, :], taps_ref[row_shift])
        summed_ref[:, lanes] = total

    chunk = 128
    inverse = 1.0 / channels

    def normalise(step, _):
        at = pl.ds(pl.multiple_of(step * chunk, chunk), chunk)
        values = summed_ref[at, :]
        centred = values - jnp.sum(values, axis=-1, keepdims=True) * inverse
        variance = jnp.sum(centred * centred, axis=-1, keepdims=True) * inverse
        features_ref[at, :] = (centred * lax.rsqrt(variance + 1e-05)).astype(BF16)
        return 0

    lax.fori_loop(0, tokens // chunk, normalise, 0)
    store = pltpu.make_async_copy(features_ref, features_hbm, load_sem.at[len(loads)])
    store.start()
    head_dim = channels // heads
    for load in loads[3:]:
        load.wait()

    def project(step, _):
        at = pl.ds(pl.multiple_of(step * BLOCK, BLOCK), BLOCK)
        keys_ref[:, at] = dot(features_ref[...], kv_ref[:, at]).astype(BF16)
        return 0

    lax.fori_loop(0, keys_ref.shape[1] // BLOCK, project, 0)

    latent_count = query_ref.shape[0]
    token_lane = lax.broadcasted_iota(jnp.int32, (tokens, LANES), 1)
    query_lane = lax.broadcasted_iota(jnp.int32, (latent_count, LANES), 1)
    token_low = token_lane < head_dim
    query_low = query_lane < head_dim
    stat_ref[...] = jnp.zeros_like(stat_ref)

    def attend(pair, _):
        at = pl.ds(pl.multiple_of(pair * LANES, LANES), LANES)
        value_at = pl.ds(pl.multiple_of(channels + pair * LANES, LANES), LANES)
        queries = query_ref[:, at]
        keys = keys_ref[:, at]
        values = keys_ref[:, value_at]
        live = live_ref[...]
        bias = (live - 1.0) * (-LOW)
        bias = bias.astype(BF16)
        ones = jnp.ones_like(values)
        results = []
        stats = stat_ref[...]
        for which in range(2):
            query_mine = query_low if which == 0 else jnp.logical_not(query_low)
            token_mine = token_low if which == 0 else jnp.logical_not(token_low)
            spot = head_dim if which == 0 else 0
            marker = (query_lane == spot).astype(F32).astype(BF16)
            query_head = jnp.where(query_mine, queries, marker)
            key_head = jnp.where(token_mine, keys, bias)
            value_head = jnp.where(token_mine, values, ones) * live
            scores = lax.dot_general(
                query_head, key_head, (((1,), (1,)), ((), ())), preferred_element_type=F32
            )
            peak = jnp.max(scores, axis=1, keepdims=True)
            weights = jnp.exp(scores - peak).astype(BF16)
            got = dot(weights, value_head)
            results.append(got)
            head = pair * 2 + which
            total = got[:, spot : spot + 1]
            stats = jnp.where(query_lane == head, peak, stats)
            stats = jnp.where(query_lane == head_dim + head, total, stats)
        stat_ref[...] = stats
        numer = jnp.where(query_low, results[0], results[1])
        denom = jnp.where(query_low, results[1], results[0])
        denom = pltpu.roll(denom, head_dim, 1)
        part_ref[:, at] = jnp.where(denom > 0, numer / jnp.maximum(denom, 1e-30), 0.0).astype(BF16)
        return 0

    lax.fori_loop(0, heads // 2, attend, 0)
    store.wait()


def local_work(borders, queries, live, pixels, patch_weight, conv_weight, kv_weight):
    tile_rows, tile_cols, patch_in = pixels.shape
    channels = patch_weight.shape[1]
    tokens = tile_rows * tile_cols
    latent_count = queries.shape[0]
    rows_ext = tile_rows + 2
    vmem = pl.BlockSpec(memory_space=pltpu.VMEM)
    leave = pl.BlockSpec(memory_space=pl.ANY)
    loaded = (
        pixels.reshape(tokens, patch_in), patch_weight, conv_weight, queries, kv_weight,
    )
    part, stat, features = pl.pallas_call(
        functools.partial(core, tile_rows, tile_cols, HEADS),
        out_shape=(
            jax.ShapeDtypeStruct((latent_count, channels), BF16),
            jax.ShapeDtypeStruct((latent_count, LANES), F32),
            jax.ShapeDtypeStruct((tokens, channels), BF16),
        ),
        in_specs=[vmem] * 5 + [leave] * len(loaded),
        out_specs=(vmem, vmem, leave),
        scratch_shapes=[pltpu.VMEM(array.shape, BF16) for array in loaded]
        + [
            pltpu.VMEM((rows_ext * tile_cols, 3 * BLOCK), BF16),
            pltpu.VMEM((3, 3 * BLOCK, BLOCK), BF16),
            pltpu.VMEM((tokens, channels), F32),
            pltpu.VMEM((tokens, 2 * channels), BF16),
            pltpu.VMEM((tokens, channels), BF16),
            pltpu.SemaphoreType.DMA((len(loaded) + 1,)),
        ],
        compiler_params=pltpu.CompilerParams(vmem_limit_bytes=60 * 1024 * 1024),
        name="local_work",
    )(*borders, live, *loaded)
    return features, part, stat


def greet(
    head_dim,
    pixels_ref, first_ref, last_ref, latent_hbm, weight_hbm,
    top_ref, bottom_ref, left_ref, right_ref, query_ref,
    latent_ref, weight_ref, send_sem, recv_sem, load_sem,
):
    loads = [
        pltpu.make_async_copy(latent_hbm, latent_ref, load_sem.at[0]),
        pltpu.make_async_copy(weight_hbm, weight_ref, load_sem.at[1]),
    ]
    for load in loads:
        load.start()
    channels = query_ref.shape[1]
    tile_rows, tile_cols, _ = pixels_ref.shape
    row_count, col_count = lax.axis_size("rows"), lax.axis_size("cols")
    row, col = lax.axis_index("rows"), lax.axis_index("cols")
    low, high = slice(0, CORNER), slice(tile_cols - CORNER, tile_cols)
    column = slice(0, tile_rows)
    above = slice(tile_rows, tile_rows + CORNER)
    below = slice(tile_rows + CORNER, tile_rows + 2 * CORNER)
    end = tile_rows - 1
    moves = (
        (1, 0, pixels_ref.at[end], top_ref),
        (-1, 0, pixels_ref.at[0], bottom_ref),
        (0, 1, last_ref, left_ref.at[column]),
        (0, -1, first_ref, right_ref.at[column]),
        (1, 1, pixels_ref.at[end, high], left_ref.at[above]),
        (1, -1, pixels_ref.at[end, low], right_ref.at[above]),
        (-1, 1, pixels_ref.at[0, high], left_ref.at[below]),
        (-1, -1, pixels_ref.at[0, low], right_ref.at[below]),
    )

    def inside(down, across):
        ok = None
        for at, step, count in ((row, down, row_count), (col, across, col_count)):
            if step:
                here = at + step < count if step > 0 else at + step >= 0
                ok = here if ok is None else jnp.logical_and(ok, here)
        return ok

    barrier = pltpu.get_barrier_semaphore()
    for down, across, _, _ in moves:
        @pl.when(inside(down, across))
        def _(down=down, across=across):
            pl.semaphore_signal(
                barrier, inc=1, device_id=(row + down, col + across), device_id_type=MESH
            )
    tall = 1 + (row > 0).astype(jnp.int32) + (row < row_count - 1).astype(jnp.int32)
    wide = 1 + (col > 0).astype(jnp.int32) + (col < col_count - 1).astype(jnp.int32)
    pl.semaphore_wait(barrier, tall * wide - 1)

    def make(number):
        down, across, source, target = moves[number]
        return pltpu.make_async_remote_copy(
            src_ref=source, dst_ref=target,
            send_sem=send_sem.at[number], recv_sem=recv_sem.at[number],
            device_id=(row + down, col + across), device_id_type=MESH,
        )

    for number, (down, across, _, _) in enumerate(moves):
        @pl.when(inside(down, across))
        def _(number=number):
            make(number).start()
    for load in loads:
        load.wait()

    def ask(step, _):
        at = pl.ds(pl.multiple_of(step * BLOCK, BLOCK), BLOCK)
        asked = dot(latent_ref[...], weight_ref[:, at]).astype(BF16).astype(F32)
        query_ref[:, at] = (asked * head_dim ** -0.5).astype(BF16)
        return 0

    lax.fori_loop(0, channels // BLOCK, ask, 0)
    for number, (down, across, _, target) in enumerate(moves):
        @pl.when(inside(-down, -across))
        def _(number=number):
            make(number).wait_recv()

        @pl.when(jnp.logical_not(inside(-down, -across)))
        def _(target=target):
            target[...] = jnp.zeros(target.shape, BF16)
    for number, (down, across, _, _) in enumerate(moves):
        @pl.when(inside(down, across))
        def _(number=number):
            make(number).wait_send()


def borders_of(pixels, latents, query_weight):
    tile_rows, tile_cols, patch_in = pixels.shape
    vmem = pl.BlockSpec(memory_space=pltpu.VMEM)
    flat = jax.ShapeDtypeStruct((tile_cols, patch_in), BF16)
    tall = jax.ShapeDtypeStruct((tile_rows + 2 * CORNER, patch_in), BF16)
    channels = query_weight.shape[1]
    leave = pl.BlockSpec(memory_space=pl.ANY)
    *borders, queries = pl.pallas_call(
        functools.partial(greet, channels // HEADS),
        out_shape=(flat, flat, tall, tall, jax.ShapeDtypeStruct((latents.shape[0], channels), BF16)),
        in_specs=[leave, vmem, vmem, leave, leave],
        out_specs=(vmem,) * 5,
        scratch_shapes=[
            pltpu.VMEM(latents.shape, BF16),
            pltpu.VMEM(query_weight.shape, BF16),
            pltpu.SemaphoreType.DMA((8,)),
            pltpu.SemaphoreType.DMA((8,)),
            pltpu.SemaphoreType.DMA((2,)),
        ],
        compiler_params=pltpu.CompilerParams(
            collective_id=2, has_side_effects=True, vmem_limit_bytes=60 * 1024 * 1024
        ),
        name="borders",
    )(pixels, pixels[:, 0], pixels[:, -1], latents, query_weight)
    return borders, queries


def spread(values, heads, head_dim, low):
    return [
        jnp.where(low, values[:, 2 * pair : 2 * pair + 1], values[:, 2 * pair + 1 : 2 * pair + 2])
        for pair in range(heads // 2)
    ]


def blend(parts, stats, heads, head_dim):
    rows = parts[0].shape[0]
    lane = lax.broadcasted_iota(jnp.int32, (rows, LANES), 1)
    low = lane < head_dim
    peaks = stats
    totals = [pltpu.roll(stat, LANES - head_dim, 1) for stat in stats]
    top = functools.reduce(jnp.maximum, peaks)
    shares = [jnp.exp(peak - top) * total for peak, total in zip(peaks, totals)]
    whole = functools.reduce(jnp.add, shares)
    inverse = jnp.where(whole > 0, 1.0 / jnp.maximum(whole, 1e-30), 0.0)
    columns = [0.0] * (heads // 2)
    for part, share in zip(parts, shares):
        factors = spread(share * inverse, heads, head_dim, low)
        for pair in range(heads // 2):
            piece = part[:, pair * LANES : (pair + 1) * LANES].astype(F32)
            columns[pair] = columns[pair] + factors[pair] * piece
    used = lane < heads
    stat = jnp.where(used, top, 0.0)
    stat = jnp.where(lane < head_dim, stat, pltpu.roll(jnp.where(used, whole, 0.0), head_dim, 1))
    return columns, stat


def exchange(
    heads,
    part_ref, stat_ref, weight_hbm,
    out_ref,
    part_one, stat_one, sum_one, tot_one, part_two, stat_two, sum_two, tot_two,
    part_three, stat_three, part_own, stat_own, weight_ref, send_sem, recv_sem, load_sem,
):
    row_count, half, _, own, channels = part_ref.shape
    head_dim = channels // heads
    row = lax.axis_index("rows")
    col = lax.axis_index("cols")
    side = lax.rem(col, 2)
    slot = lax.div(col, 2)
    mine = [
        pltpu.make_async_copy(part_ref.at[:, :, side], part_own, load_sem.at[0]),
        pltpu.make_async_copy(stat_ref.at[:, :, side], stat_own, load_sem.at[1]),
    ]
    load = pltpu.make_async_copy(weight_hbm, weight_ref, load_sem.at[2])
    for copy in mine:
        copy.start()

    twin = (row, slot * 2 + (1 - side))
    row_peers = [(lax.rem(row + step, row_count), col) for step in range(1, row_count)]
    col_peers = [(row, lax.rem(slot + step, half) * 2 + side) for step in range(1, half)]
    barrier = pltpu.get_barrier_semaphore()
    for peer in [twin] + row_peers + col_peers:
        pl.semaphore_signal(barrier, inc=1, device_id=peer, device_id_type=MESH)
    pl.semaphore_wait(barrier, 1 + len(row_peers) + len(col_peers))

    def send(source, target, peer, number):
        copy = pltpu.make_async_remote_copy(
            src_ref=source, dst_ref=target,
            send_sem=send_sem.at[number], recv_sem=recv_sem.at[number],
            device_id=peer, device_id_type=MESH,
        )
        copy.start()
        return copy

    row_order = [lax.rem(row + step, row_count) for step in range(1, row_count + 1)]
    col_order = [lax.rem(slot + step, half) for step in range(1, half + 1)]
    ones, twos, threes = [], [], []
    for step, a in enumerate(row_order):
        ones.append(
            (
                send(part_ref.at[a, :, 1 - side], part_one.at[a], twin, 2 * step),
                send(stat_ref.at[a, :, 1 - side], stat_one.at[a], twin, 2 * step + 1),
            )
        )
    load.start()
    for copy in mine:
        copy.wait()
    number = 2 * row_count
    for step, a in enumerate(row_order):
        for copy in ones[step]:
            copy.wait_recv()

        def first(b, _, a=a):
            columns, stat = blend(
                [part_own[a, b], part_one[a, b]], [stat_own[a, b], stat_one[a, b]],
                heads, head_dim,
            )
            for pair, column in enumerate(columns):
                sum_one[a, b, :, pair * LANES : (pair + 1) * LANES] = column.astype(BF16)
            tot_one[a, b] = stat
            return 0

        lax.fori_loop(0, half, first, 0)
        if step < row_count - 1:
            twos.append(send(sum_one.at[a], part_two.at[step], row_peers[step], number))
            twos.append(send(tot_one.at[a], stat_two.at[step], row_peers[step], number + 1))
            number += 2
    for copy in twos:
        copy.wait_recv()
    for step, b in enumerate(col_order):
        columns, stat = blend(
            [sum_one[row, b]] + [part_two[other, b] for other in range(row_count - 1)],
            [tot_one[row, b]] + [stat_two[other, b] for other in range(row_count - 1)],
            heads, head_dim,
        )
        if step < half - 1:
            for pair, column in enumerate(columns):
                sum_two[b, :, pair * LANES : (pair + 1) * LANES] = column.astype(BF16)
            tot_two[b] = stat
            threes.append(send(sum_two.at[b], part_three.at[step], col_peers[step], number))
            threes.append(send(tot_two.at[b], stat_three.at[step], col_peers[step], number + 1))
            number += 2
    for copy in threes:
        copy.wait_recv()
    columns, _ = blend(
        [jnp.concatenate(columns, 1)] + [part_three[step] for step in range(half - 1)],
        [stat] + [stat_three[step] for step in range(half - 1)],
        heads, head_dim,
    )
    for copy in [copy for both in ones for copy in both] + twos + threes:
        copy.wait_send()
    attended = jnp.concatenate(columns, 1)
    mean = jnp.sum(attended * attended, axis=-1, keepdims=True) * (1.0 / channels)
    normed = (attended * lax.rsqrt(mean + 1e-06)).astype(BF16)
    load.wait()
    out_ref[...] = dot(normed, weight_ref[...]).astype(BF16)


def combine(part, stat, out_weight):
    row_count, col_count = lax.axis_size("rows"), lax.axis_size("cols")
    half = col_count // 2
    latent_count, channels = part.shape
    own = latent_count // (row_count * col_count)
    part = part.reshape(row_count, half, 2, own, channels)
    stat = stat.reshape(row_count, half, 2, own, LANES)
    vmem = pl.BlockSpec(memory_space=pltpu.VMEM)
    copies = 2 * (2 * row_count - 1) + 2 * (half - 1)

    def pairs(*extent):
        return [
            pltpu.VMEM(extent + (own, channels), BF16), pltpu.VMEM(extent + (own, LANES), F32)
        ]

    return pl.pallas_call(
        functools.partial(exchange, HEADS),
        out_shape=jax.ShapeDtypeStruct((own, out_weight.shape[1]), BF16),
        in_specs=[pl.BlockSpec(memory_space=pl.ANY)] * 3,
        out_specs=vmem,
        scratch_shapes=pairs(row_count, half)
        + pairs(row_count, half)
        + pairs(row_count - 1, half)
        + pairs(half)
        + pairs(half - 1)
        + pairs(row_count, half)
        + [
            pltpu.VMEM(out_weight.shape, BF16),
            pltpu.SemaphoreType.DMA((copies,)),
            pltpu.SemaphoreType.DMA((copies,)),
            pltpu.SemaphoreType.DMA((3,)),
        ],
        compiler_params=pltpu.CompilerParams(
            collective_id=1, has_side_effects=True, vmem_limit_bytes=60 * 1024 * 1024
        ),
        name="combine",
    )(part, stat, out_weight)


def shards(pixels, tissue, patch_weight, conv_weight, kv_weight, query_weight, out_weight, latents):
    tile_rows, tile_cols, _ = pixels.shape
    channels = patch_weight.shape[1]
    tokens = tile_rows * tile_cols
    live = jnp.broadcast_to((tissue.reshape(tokens, 1) > 0).astype(BF16), (tokens, LANES))
    borders, queries = borders_of(pixels, latents, query_weight)
    features, part, stat = local_work(
        borders, queries, live, pixels, patch_weight, conv_weight, kv_weight
    )
    latents_out = combine(part, stat, out_weight)
    return (features.reshape(tile_rows, tile_cols, channels), latents_out)


def solution(mesh):
    return jax.shard_map(
        shards,
        mesh=mesh,
        in_specs=(P("rows", "cols", None), P("rows", "cols"), P(), P(), P(), P(), P(), P()),
        out_specs=(P("rows", "cols", None), P(("rows", "cols"), None)),
        check_vma=False,
    )
```
